512 devices in a mesh: dp: 16 (over x, z_hi), tm: 32 (over z_lo, y, core).
Axes of the slice: x: 4, y: 8, z: 8 (z_hi: 4, z_lo: 2; z = z_hi * 2 + z_lo), core: 2. Of those that a mesh axis runs over, the one named last changes fastest.
Arguments:
- activations: bfloat16 [16, 64, 64, 16, 128], P('dp', 'tm')
- conv_weight: bfloat16 [3, 3, 3, 128, 128], replicated, may hold values from -0.109375 to 0.109375
- norm_gain: float32 [128], replicated, may hold values from 0.5 to 1.5
- norm_bias: float32 [128], replicated, may hold values from -0.5 to 0.5
- down_weight: bfloat16 [3, 3, 128, 128], replicated, may hold values from -0.1875 to 0.1875
- cotangent: bfloat16 [16, 64, 32, 8, 128], P('dp', None, 'tm'), may hold values from -0.21875 to 0.21875
Outputs:
- encoded: bfloat16 [16, 64, 32, 8, 128], P('dp', None, 'tm')
- grad_down: float32 [3, 3, 128, 128], P(None, None, None, 'tm')
The draws below stay inside these ranges and needn't reach their ends.
All inputs are finite; a program needn't handle non-finite values.
Results may differ from the reference program's by a relative error of at most 0.005.
Values may be sent and summed in bfloat16 or wider, within the bound.
A program may use at most 64 MiB of HBM per device.

```python
import math
import jax
import jax.numpy as jnp
from jax import lax

C = 128
C2 = 128
G = 32
H = 64
W = 16
CLIPS = 16
FRAMES = 64
H2 = 32
W2 = 8


def draw_activations(key, part):
    key_base = jax.random.fold_in(key, 0)
    key_chan = jax.random.fold_in(key, 1)
    key_frames = jax.random.fold_in(key, 3)
    key_flip = jax.random.fold_in(key, 4)
    shape = (CLIPS, FRAMES, H, W, C)
    position = jnp.arange(FRAMES).astype(jnp.float32) / float(max(FRAMES - 1, 1))
    flipped = jax.random.bernoulli(key_flip, 0.5, (CLIPS, 1))
    ramp = jnp.where(flipped, 1.0 - position[None, :], position[None, :])
    jitter = jax.random.uniform(key_frames, (CLIPS, FRAMES), jnp.float32, 0.0, math.log(10.0))
    frame_scale = jnp.exp(ramp * math.log(3.0) + jitter)
    chan_scale = jnp.exp(jax.random.uniform(key_chan, (C,), jnp.float32, 0.0, math.log(10.0)))
    base = jnp.clip(jax.random.normal(key_base, shape, jnp.float32), -6.0, 6.0)
    values = base * frame_scale[:, :, None, None, None] * chan_scale
    return values.astype(jnp.bfloat16)


def strengthened(values, stream_key, source, target, blocks, factor):
    owner, partner = [(jnp.arange(values.shape[dim]) // (values.shape[dim] // blocks)).reshape([-1 if axis == dim else 1 for axis in range(values.ndim)]) for dim in (source, target)]
    chosen = jax.random.permutation(stream_key, blocks)[partner]
    strong = (owner == chosen) | (owner == (partner + blocks // 2) % blocks)
    return jnp.where(strong, factor * values, values)


def block_levels(stream_key, shape, shards, low, top_value):
    loudness, own = 1.0, jax.random.fold_in(stream_key, 6)
    for dim, shards_of in shards:
        steps = jnp.exp(jax.random.uniform(jax.random.fold_in(own, dim), (shards_of,), jnp.float32, low / len(shards), top_value / len(shards)))
        loudness = loudness * jnp.repeat(steps, shape[dim] // shards_of).reshape([-1 if axis == dim else 1 for axis in range(len(shape))])
    return loudness


def scatter_about(rng, dims, spread, bound, cuts=(), dtype=jnp.bfloat16):
    entries = jax.random.normal(rng, dims, jnp.float32) * spread
    if len(cuts) > 0:
        entries = block_levels(rng, dims, cuts, -0.22, 0.18) * entries
    return jnp.clip(entries, min=-bound, max=bound).astype(dtype)


def heavy_noise(rng, extent, scale, most, pieces, heavy, kind=jnp.bfloat16):
    values = scale * jax.random.normal(rng, extent, jnp.float32)
    if pieces:
        values = values * block_levels(rng, extent, pieces, -0.22, 0.18)
    return jnp.clip(strengthened(values, jax.random.fold_in(rng, 3), *heavy), -most, most).astype(kind)


def setup_inputs(seed: int = 0) -> dict:
    keys = jax.random.split(jax.random.key(seed), 7)
    return {
        "activations": draw_activations(jax.random.fold_in(keys[6], 71), 0),
        "conv_weight": scatter_about(keys[1], (3, 3, 3, C, C), (27 * C) ** -0.5, 0.109375),
        "norm_gain": jnp.clip(jax.random.uniform(keys[2], (C,), jnp.float32, 0.5, 1.5), 0.5, 1.5),
        "norm_bias": jnp.clip(jax.random.uniform(keys[3], (C,), jnp.float32, -0.5, 0.5), -0.5, 0.5),
        "down_weight": scatter_about(keys[4], (3, 3, C, C2), (9 * C) ** -0.5, 0.1875),
        "cotangent": heavy_noise(keys[5], (CLIPS, FRAMES, H2, W2, C2), ((CLIPS * FRAMES * H2 * W2) ** -0.5 * 4), 0.21875, ((0, 16), (2, 32)), (2, 4, 32, 2.75)),
    }


def clip_pass(inputs, grad_out, conv_weight, norm_gain, norm_bias, down_weight):
    inputs_f32 = inputs.astype(jnp.float32)[None]
    conv_out = lax.conv_general_dilated(inputs_f32, conv_weight.astype(jnp.float32), (1, 1, 1), [(2, 0), (1, 1), (1, 1)], dimension_numbers=('NDHWC', 'DHWIO', 'NDHWC'), precision=lax.Precision.HIGHEST)[0]
    grouped = conv_out.reshape(FRAMES, H, W, G, C // G)
    members = float(FRAMES * H * W * (C // G))
    group_sums = lax.optimization_barrier(jnp.sum(grouped, axis=(0, 1, 2, 4)))
    group_squares = lax.optimization_barrier(jnp.sum(grouped * grouped, axis=(0, 1, 2, 4)))
    group_mean = group_sums / members
    variance = group_squares / members - group_mean * group_mean
    inverse = lax.rsqrt(variance + 1e-06)
    normed = ((grouped - group_mean[:, None]) * inverse[:, None]).reshape(FRAMES, H, W, C) * norm_gain + norm_bias
    hidden = jax.nn.silu(normed).astype(jnp.bfloat16)
    hidden_f32 = hidden.astype(jnp.float32)

    def down_conv(weights):
        return lax.conv_general_dilated(hidden_f32, weights, (2, 2), [(0, 1), (0, 1)], dimension_numbers=('NHWC', 'HWIO', 'NHWC'), precision=lax.Precision.HIGHEST)
    encoded_clip, pullback = jax.vjp(down_conv, down_weight.astype(jnp.float32))
    grad_clip, = pullback(grad_out.astype(jnp.float32))
    return (encoded_clip.astype(jnp.bfloat16), grad_clip)

def reference(activations, conv_weight, norm_gain, norm_bias, down_weight, cotangent):

    def one_clip(pair):
        return clip_pass(pair[0], pair[1], conv_weight, norm_gain, norm_bias, down_weight)
    encoded, grads = lax.map(one_clip, (activations, cotangent))
    return (encoded, lax.optimization_barrier(jnp.sum(grads, axis=0)))
```

```python
import jax
import jax.numpy as jnp
from jax import lax
from jax.sharding import PartitionSpec as P

G = 32


def passed_along(shard, axis, by):
    count = lax.axis_size(axis)
    pairs = [(i, i + by) for i in range(count) if 0 <= i + by < count]
    return lax.ppermute(shard, axis, pairs)


def from_all(value, axis):
    count = lax.axis_size(axis)
    copies = jnp.broadcast_to(value[None], (count, *value.shape))
    return lax.all_to_all(copies, axis, split_axis=0, concat_axis=0, tiled=True)


def per_device(activations, conv_weight, norm_gain, norm_bias, down_weight, cotangent):
    clip_count, frames_dev, height, width_cells, channels = activations.shape
    out_channels = conv_weight.shape[-1]
    members_tm = lax.axis_size("tm")
    groups = G
    per_group = channels // groups
    earlier = passed_along(activations, "tm", 1)
    cot = lax.all_to_all(cotangent, "tm", split_axis=1, concat_axis=2, tiled=True)
    framed = jnp.concatenate([earlier, activations], axis=1)
    framed = jnp.pad(framed, ((0, 0), (0, 0), (1, 1), (1, 1), (0, 0)))
    conv_out = jnp.zeros(
        (clip_count * frames_dev * height * width_cells, out_channels), jnp.float32
    )
    for row_tap in range(3):
        for col_tap in range(3):
            window_slab = framed[
                :, :, row_tap : row_tap + height, col_tap : col_tap + width_cells, :
            ]
            stacked = jnp.concatenate(
                [window_slab[:, time_tap : time_tap + frames_dev] for time_tap in range(3)], axis=-1
            )
            tap_weight = conv_weight[:, row_tap, col_tap].reshape(3 * channels, out_channels)
            conv_out = conv_out + jnp.dot(
                stacked.reshape(-1, 3 * channels), tap_weight, preferred_element_type=jnp.float32
            )
    sums = jnp.stack([jnp.sum(conv_out, axis=0), jnp.sum(conv_out * conv_out, axis=0)])
    sums = jnp.sum(from_all(sums, "tm"), axis=0)
    group_sums, group_squares = jnp.sum(sums.reshape(2, groups, per_group), axis=-1)
    members = float(frames_dev * members_tm * height * width_cells * per_group)
    group_mean = group_sums / members
    variance = group_squares / members - group_mean * group_mean
    inverse = lax.rsqrt(variance + 1e-06)
    mean_c = jnp.repeat(group_mean, per_group)
    inverse_c = jnp.repeat(inverse, per_group)
    normed = (conv_out - mean_c) * inverse_c * norm_gain + norm_bias
    hidden = jax.nn.silu(normed).astype(jnp.bfloat16)
    hidden = hidden.reshape(frames_dev, height, width_cells, channels)
    extended = jnp.pad(hidden, ((0, 0), (0, 1), (0, 1), (0, 0)))
    rows_out, cols_out = height // 2, width_cells // 2
    patches = jnp.concatenate(
        [
            extended[
                :, p : p + 2 * rows_out - 1 : 2, q : q + 2 * cols_out - 1 : 2, :
            ]
            for p in range(3)
            for q in range(3)
        ],
        axis=-1,
    ).reshape(-1, 9 * channels)
    encoded = (
        jnp.dot(patches, down_weight.reshape(9 * channels, -1), preferred_element_type=jnp.float32)
        .astype(jnp.bfloat16)
        .reshape(clip_count, frames_dev, rows_out, cols_out, out_channels)
    )
    encoded = lax.all_to_all(encoded, "tm", split_axis=2, concat_axis=1, tiled=True)
    partial_value = lax.dot_general(
        cot.reshape(-1, out_channels),
        patches,
        (((0,), (0,)), ((), ())),
        preferred_element_type=jnp.float32,
    )
    own = out_channels // members_tm
    shares = partial_value.reshape(members_tm, own, 9 * channels)
    shares = lax.all_to_all(shares, "tm", split_axis=0, concat_axis=0, tiled=True)
    shares = jnp.sum(shares, axis=0)
    total = jnp.sum(from_all(shares, "dp"), axis=0)
    grad_down = total.T.reshape(3, 3, channels, own)
    return (encoded, grad_down)


def solution(mesh):
    placed = (P("dp", "tm", None, None, None), P(), P(), P(), P(), P("dp", None, "tm", None, None))
    return jax.shard_map(
        per_device,
        mesh=mesh,
        in_specs=placed,
        out_specs=(P("dp", None, "tm", None, None), P(None, None, None, "tm")),
        check_vma=False,
    )
```

```python
import functools

import jax
import jax.numpy as jnp
from jax import lax
from jax.experimental import pallas as pl
from jax.experimental.pallas import tpu as pltpu
from jax.sharding import PartitionSpec as P

GROUP_SIZE = 4
MESH = pl.DeviceIdType.MESH
Z_PART = 4
VMEM = pl.BlockSpec(memory_space=pltpu.VMEM)


def passed_along(shard, axis, by):
    count = lax.axis_size(axis)
    pairs = [(i, i + by) for i in range(count) if 0 <= i + by < count]
    return lax.ppermute(shard, axis, pairs)


def conv_kernel(height, width, earlier_ref, now_ref, weight_ref, out_ref, lanes_ref, wide_ref):
    cells = height * width
    c = 128
    edge = jnp.zeros((width, 4 * c), jnp.bfloat16)
    lanes_ref[pl.ds(0, width), :] = edge
    lanes_ref[pl.ds(cells + width, width), :] = edge
    for frame in range(4):
        source = earlier_ref if frame < 2 else now_ref
        lanes_ref[pl.ds(width, cells), frame * c : (frame + 1) * c] = source[frame % 2]
    zero = jnp.zeros((c, c), jnp.bfloat16)
    for p in range(3):
        for frame in range(4):
            for t in range(2):
                for q in range(3):
                    a = frame - t
                    block = weight_ref[a, p, q] if 0 <= a <= 2 else zero
                    column = (t * 3 + q) * c
                    wide_ref[p, frame * c : (frame + 1) * c, column : column + c] = block
    rows = 16 * width
    column = lax.broadcasted_iota(jnp.int32, (rows, c), 0) % width

    def chunk(step, carry):
        start = pl.multiple_of(step * rows, rows)
        z = jnp.zeros((rows, 6 * c), jnp.float32)
        for p in range(3):
            z = z + jnp.dot(
                lanes_ref[pl.ds(pl.multiple_of(start + p * width, width), rows), :],
                wide_ref[p],
                preferred_element_type=jnp.float32,
            )
        for t in range(2):
            left, middle, right = (z[:, (t * 3 + q) * c : (t * 3 + q + 1) * c] for q in range(3))
            left = jnp.where(column == 0, 0.0, pltpu.roll(left, 1, 0))
            right = jnp.where(column == width - 1, 0.0, pltpu.roll(right, rows - 1, 0))
            out_ref[pl.ds(pl.multiple_of(t * cells + start, rows), rows), :] = left + middle + right
        return carry

    lax.fori_loop(0, height // 16, chunk, 0)


def mid_kernel(
    n_tm, n_dp, height, width, piece,
    conv_ref, gain_ref, bias_ref, down_ref, cot_ref,
    enc_out, grad_out,
    stat_src, stat_buf, patches, enc_src, enc_buf, grad_all, grad_wide, grad_src, grad_buf,
    x_src, x_buf, z_src, z_buf,
    stat_send, stat_recv, enc_send, enc_recv, grad_send, grad_recv, x_send, x_recv, z_send, z_recv,
):
    c = 128
    own = c // n_tm
    n_x = n_dp // Z_PART
    me = lax.axis_index("tm")
    dp = lax.axis_index("dp")
    my_x, my_z = dp // Z_PART, dp % Z_PART

    def tm_peer(d):
        return {"tm": lax.rem(me + d, n_tm)}

    def x_peer(d):
        return {"dp": lax.rem(my_x + d, n_x) * Z_PART + my_z}

    def z_peer(d):
        return {"dp": my_x * Z_PART + lax.rem(my_z + d, Z_PART)}

    barrier = pltpu.get_barrier_semaphore()

    def greet(d, carry):
        pl.semaphore_signal(barrier, inc=1, device_id=tm_peer(d), device_id_type=MESH)
        return carry

    lax.fori_loop(1, n_tm, greet, 0)
    for d in range(1, n_x):
        pl.semaphore_signal(barrier, inc=1, device_id=x_peer(d), device_id_type=MESH)
    for d in range(1, Z_PART):
        pl.semaphore_signal(barrier, inc=1, device_id=z_peer(d), device_id_type=MESH)

    conv = conv_ref[...]
    local = jnp.concatenate(
        [
            jnp.sum(conv, axis=0, keepdims=True),
            jnp.sum(conv * conv, axis=0, keepdims=True),
            jnp.zeros((6, c), jnp.float32),
        ],
        axis=0,
    )
    stat_src[...] = local
    stat_buf[me] = local
    pl.semaphore_wait(barrier, n_tm - 1 + n_x - 1 + Z_PART - 1)

    def exchange(size, peer, mine, src_of, dst_of, send, recv):
        def sender(d):
            target = lax.rem(mine + d, size)
            return pltpu.make_async_remote_copy(
                src_ref=src_of(target), dst_ref=dst_of(mine), send_sem=send.at[d],
                recv_sem=recv.at[mine], device_id=peer(d), device_id_type=MESH,
            )

        def receiver(d):
            origin = lax.rem(mine + size - d, size)
            return pltpu.make_async_remote_copy(
                src_ref=src_of(origin), dst_ref=dst_of(origin), send_sem=send.at[d],
                recv_sem=recv.at[origin], device_id=peer(d), device_id_type=MESH,
            )

        def loop(act):
            def step(d, carry):
                act(d)
                return carry

            lax.fori_loop(1, size, step, 0)

        loop(lambda d: sender(d).start())
        return (
            lambda: loop(lambda d: receiver(d).wait_recv()),
            lambda: loop(lambda d: sender(d).wait_send()),
        )

    stats_here, stats_gone = exchange(
        n_tm, tm_peer, me, lambda i: stat_src, lambda i: stat_buf.at[i], stat_send, stat_recv
    )
    stats_here()
    sums = jnp.sum(stat_buf[...], axis=0)
    lane = lax.broadcasted_iota(jnp.int32, (8, c), 1)
    for reach in (1, 2):
        partner = jnp.where(
            lane % (2 * reach) < reach, pltpu.roll(sums, c - reach, 1), pltpu.roll(sums, reach, 1)
        )
        sums = sums + partner
    members = float(n_tm * 2 * height * width * GROUP_SIZE)
    mean = sums[0:1] / members
    variance = sums[1:2] / members - mean * mean
    scale = lax.rsqrt(variance + 1e-06)
    gain, bias = gain_ref[...], bias_ref[...]

    half_w, half_h = width // 2, height // 2
    rows_half = height * half_w

    def hidden_at(parity):
        frames = []
        for t in range(2):
            x = conv_ref[pl.ds(t * height * width + parity, rows_half, stride=2), :]
            y = (x - mean) * scale * gain + bias
            y = y / (1.0 + jnp.exp(-y))
            y = y.astype(jnp.bfloat16).astype(jnp.float32)
            frames.append(y.reshape(half_h, 2, 1, half_w, c))
        return jnp.concatenate(frames, axis=2)

    even, odd = hidden_at(0), hidden_at(1)
    flat = even.reshape(-1, half_w, c)
    place = lax.broadcasted_iota(jnp.int32, flat.shape, 1)
    shifted = jnp.where(place == half_w - 1, 0.0, pltpu.roll(flat, half_w - 1, 1)).reshape(even.shape)
    for q, source in enumerate((even, odd, shifted)):
        upper, lower = source[:, 0], source[:, 1]
        below = jnp.concatenate([upper[1:], jnp.zeros_like(upper[:1])], axis=0)
        for p, rows in enumerate((upper, lower, below)):
            at = (p * 3 + q) * c
            patches[:, at : at + c] = rows.reshape(-1, c).astype(jnp.bfloat16)

    partial_grad = lax.dot_general(
        cot_ref[...], patches[...], (((0,), (0,)), ((), ())), preferred_element_type=jnp.float32
    )
    for tap in range(9):
        grad_all[tap] = partial_grad[:, tap * c : (tap + 1) * c]
    grad_wide[...] = jnp.zeros_like(grad_wide)
    for tap in range(9):
        for j in range(own):
            grad_wide[pl.ds(tap * own + j, n_tm, stride=piece), :] = grad_all[
                tap, pl.ds(j, n_tm, stride=own), :
            ]
    grad_src[...] = grad_wide[...].astype(jnp.bfloat16)
    grad_here, grad_gone = exchange(
        n_tm, tm_peer, me,
        lambda i: grad_src.at[pl.ds(pl.multiple_of(i * piece, piece), piece)],
        lambda i: grad_buf.at[pl.ds(pl.multiple_of(i * piece, piece), piece)],
        grad_send, grad_recv,
    )
    here = pl.ds(pl.multiple_of(me * piece, piece), piece)
    grad_buf[here, :] = grad_src[here, :]

    enc = 2 * half_w
    enc_src[...] = jnp.dot(
        patches[...], down_ref[...], preferred_element_type=jnp.float32
    ).astype(jnp.bfloat16)
    enc_here, enc_gone = exchange(
        n_tm, tm_peer, me,
        lambda i: enc_src.at[pl.ds(pl.multiple_of(i * enc, enc), enc)],
        lambda i: enc_buf.at[pl.ds(pl.multiple_of(i * enc, enc), enc)],
        enc_send, enc_recv,
    )
    mine = pl.ds(pl.multiple_of(me * enc, enc), enc)
    enc_buf[mine, :] = enc_src[mine, :]

    grad_here()
    total = jnp.zeros((piece, c), jnp.float32)
    for i in range(n_tm):
        total = total + grad_buf[pl.ds(i * piece, piece), :].astype(jnp.float32)
    x_src[...] = total
    x_buf[my_x] = total
    x_here, x_gone = exchange(
        n_x, x_peer, my_x, lambda i: x_src, lambda i: x_buf.at[i], x_send, x_recv
    )
    x_here()
    total = jnp.sum(x_buf[...], axis=0)
    z_src[...] = total
    z_buf[my_z] = total
    z_here, z_gone = exchange(
        Z_PART, z_peer, my_z, lambda i: z_src, lambda i: z_buf.at[i], z_send, z_recv
    )
    enc_here()
    enc_out[...] = enc_buf[...]
    z_here()
    grad_out[...] = jnp.sum(z_buf[...], axis=0)
    for gone in (stats_gone, grad_gone, enc_gone, x_gone, z_gone):
        gone()


def per_device(activations, conv_weight, norm_gain, norm_bias, down_weight, cotangent):
    _, frames_dev, height, width, c = activations.shape
    n_tm, n_dp = lax.axis_size("tm"), lax.axis_size("dp")
    cells = height * width
    positions = frames_dev * cells // 4
    own = c // n_tm
    piece = -(-9 * own // 16) * 16
    earlier = passed_along(activations, "tm", 1)
    cot = lax.all_to_all(
        cotangent.reshape(positions, c), "tm", split_axis=0, concat_axis=0, tiled=True
    )
    conv_out = pl.pallas_call(
        functools.partial(conv_kernel, height, width),
        out_shape=jax.ShapeDtypeStruct((frames_dev * cells, c), jnp.float32),
        in_specs=[VMEM] * 3,
        out_specs=VMEM,
        scratch_shapes=[
            pltpu.VMEM((cells + 2 * width, 4 * c), jnp.bfloat16),
            pltpu.VMEM((3, 4 * c, 6 * c), jnp.bfloat16),
        ],
        name="causal_conv",
    )(
        earlier.reshape(frames_dev, cells, c), activations.reshape(frames_dev, cells, c), conv_weight
    )
    f32, bf16 = jnp.float32, jnp.bfloat16
    n_x = n_dp // Z_PART
    dma = pltpu.SemaphoreType.DMA
    encoded, grad = pl.pallas_call(
        functools.partial(mid_kernel, n_tm, n_dp, height, width, piece),
        out_shape=(
            jax.ShapeDtypeStruct((positions, c), bf16),
            jax.ShapeDtypeStruct((piece, c), f32),
        ),
        in_specs=[VMEM] * 5,
        out_specs=(VMEM, VMEM),
        scratch_shapes=[
            pltpu.VMEM((8, c), f32),
            pltpu.VMEM((n_tm, 8, c), f32),
            pltpu.VMEM((positions, 9 * c), bf16),
            pltpu.VMEM((positions, c), bf16),
            pltpu.VMEM((positions, c), bf16),
            pltpu.VMEM((9, c, c), f32),
            pltpu.VMEM((n_tm * piece, c), f32),
            pltpu.VMEM((n_tm * piece, c), bf16),
            pltpu.VMEM((n_tm * piece, c), bf16),
            pltpu.VMEM((piece, c), f32),
            pltpu.VMEM((n_x, piece, c), f32),
            pltpu.VMEM((piece, c), f32),
            pltpu.VMEM((Z_PART, piece, c), f32),
        ]
        + [dma((n_tm,))] * 6
        + [dma((n_x,))] * 2
        + [dma((Z_PART,))] * 2,
        compiler_params=pltpu.CompilerParams(collective_id=0, has_side_effects=True),
        name="norm_down_grad",
    )(
        conv_out,
        norm_gain.reshape(1, c),
        norm_bias.reshape(1, c),
        down_weight.reshape(9 * c, c),
        cot,
    )
    grad_down = grad[: 9 * own].reshape(9, own, c).transpose(0, 2, 1).reshape(3, 3, c, own)
    return encoded.reshape(cotangent.shape), grad_down


def solution(mesh):
    placed = (P("dp", "tm", None, None, None), P(), P(), P(), P(), P("dp", None, "tm", None, None))
    return jax.shard_map(
        per_device,
        mesh=mesh,
        in_specs=placed,
        out_specs=(P("dp", None, "tm", None, None), P(None, None, None, "tm")),
        check_vma=False,
    )
```

```python
import functools

import jax
import jax.numpy as jnp
from jax import lax
from jax.experimental import pallas as pl
from jax.experimental.pallas import tpu as pltpu
from jax.sharding import PartitionSpec as P

GROUP_SIZE = 4
MESH = pl.DeviceIdType.MESH
Z_PART = 4
VMEM = pl.BlockSpec(memory_space=pltpu.VMEM)


def passed_along(shard, axis, by):
    count = lax.axis_size(axis)
    pairs = [(i, i + by) for i in range(count) if 0 <= i + by < count]
    return lax.ppermute(shard, axis, pairs)


def convolve(height, width, earlier_ref, now_ref, weight_ref, out_ref, lanes_ref, wide_ref):
    cells = height * width
    c = 128
    edge = jnp.zeros((width, 4 * c), jnp.bfloat16)
    lanes_ref[pl.ds(0, width), :] = edge
    lanes_ref[pl.ds(cells + width, width), :] = edge
    for frame in range(4):
        source = earlier_ref if frame < 2 else now_ref
        lanes_ref[pl.ds(width, cells), frame * c : (frame + 1) * c] = source[frame % 2]
    zero = jnp.zeros((c, c), jnp.bfloat16)
    for p in range(3):
        for frame in range(4):
            for t in range(2):
                for q in range(3):
                    a = frame - t
                    block = weight_ref[a, p, q] if 0 <= a <= 2 else zero
                    column = (t * 3 + q) * c
                    wide_ref[p, frame * c : (frame + 1) * c, column : column + c] = block
    rows = 16 * width
    column = lax.broadcasted_iota(jnp.int32, (rows, c), 0) % width

    def chunk(step, carry):
        sums, squares = carry
        start = pl.multiple_of(step * rows, rows)
        z = jnp.zeros((rows, 6 * c), jnp.float32)
        for p in range(3):
            z = z + jnp.dot(
                lanes_ref[pl.ds(pl.multiple_of(start + p * width, width), rows), :],
                wide_ref[p],
                preferred_element_type=jnp.float32,
            )
        for t in range(2):
            left, middle, right = (z[:, (t * 3 + q) * c : (t * 3 + q + 1) * c] for q in range(3))
            left = jnp.where(column == 0, 0.0, pltpu.roll(left, 1, 0))
            right = jnp.where(column == width - 1, 0.0, pltpu.roll(right, rows - 1, 0))
            value = left + middle + right
            out_ref[pl.ds(pl.multiple_of(t * cells + start, rows), rows), :] = value
            value = value.reshape(rows // 8, 8, c)
            sums = sums + jnp.sum(value, axis=0)
            squares = squares + jnp.sum(value * value, axis=0)
        return sums, squares

    none = jnp.zeros((8, c), jnp.float32)
    return lax.fori_loop(0, height // 16, chunk, (none, none))


def block_kernel(
    n_tm, n_dp, height, width, piece,
    earlier_ref, now_ref, weight_ref, gain_ref, bias_ref, down_ref, cot_src,
    enc_out, grad_out,
    lanes_ref, wide_ref, conv_ref, cot_ref, stat_src, stat_buf, patches, enc_src, enc_buf, grad_all, grad_wide, grad_src, grad_buf,
    x_src, x_buf, z_src, z_buf,
    stat_send, stat_recv, cot_send, cot_recv, enc_send, enc_recv, grad_send, grad_recv, x_send, x_recv, z_send, z_recv,
):
    c = 128
    own = c // n_tm
    n_x = n_dp // Z_PART
    me = lax.axis_index("tm")
    dp = lax.axis_index("dp")
    my_x, my_z = dp // Z_PART, dp % Z_PART

    def tm_peer(d):
        return {"tm": lax.rem(me + d, n_tm)}

    def x_peer(d):
        return {"dp": lax.rem(my_x + d, n_x) * Z_PART + my_z}

    def z_peer(d):
        return {"dp": my_x * Z_PART + lax.rem(my_z + d, Z_PART)}

    barrier = pltpu.get_barrier_semaphore()

    def greet(d, carry):
        pl.semaphore_signal(barrier, inc=1, device_id=tm_peer(d), device_id_type=MESH)
        return carry

    lax.fori_loop(1, n_tm, greet, 0)
    for d in range(1, n_x):
        pl.semaphore_signal(barrier, inc=1, device_id=x_peer(d), device_id_type=MESH)
    for d in range(1, Z_PART):
        pl.semaphore_signal(barrier, inc=1, device_id=z_peer(d), device_id_type=MESH)

    own_sums, own_squares = convolve(
        height, width, earlier_ref, now_ref, weight_ref, conv_ref, lanes_ref, wide_ref
    )
    local = jnp.concatenate(
        [
            jnp.sum(own_sums, axis=0, keepdims=True),
            jnp.sum(own_squares, axis=0, keepdims=True),
            jnp.zeros((6, c), jnp.float32),
        ],
        axis=0,
    )
    stat_src[...] = local
    stat_buf[me] = local
    pl.semaphore_wait(barrier, n_tm - 1 + n_x - 1 + Z_PART - 1)

    def exchange(size, peer, mine, src_of, dst_of, send, recv):
        def sender(d):
            target = lax.rem(mine + d, size)
            return pltpu.make_async_remote_copy(
                src_ref=src_of(target), dst_ref=dst_of(mine), send_sem=send.at[d],
                recv_sem=recv.at[mine], device_id=peer(d), device_id_type=MESH,
            )

        def receiver(d):
            origin = lax.rem(mine + size - d, size)
            return pltpu.make_async_remote_copy(
                src_ref=src_of(origin), dst_ref=dst_of(origin), send_sem=send.at[d],
                recv_sem=recv.at[origin], device_id=peer(d), device_id_type=MESH,
            )

        def loop(act):
            def step(d, carry):
                act(d)
                return carry

            lax.fori_loop(1, size, step, 0)

        loop(lambda d: sender(d).start())
        return (
            lambda: loop(lambda d: receiver(d).wait_recv()),
            lambda: loop(lambda d: sender(d).wait_send()),
        )

    stats_here, stats_gone = exchange(
        n_tm, tm_peer, me, lambda i: stat_src, lambda i: stat_buf.at[i], stat_send, stat_recv
    )
    enc = width

    def block_of(ref):
        return lambda i: ref.at[pl.ds(pl.multiple_of(i * enc, enc), enc)]

    cot_here, cot_gone = exchange(
        n_tm, tm_peer, me, block_of(cot_src), block_of(cot_ref), cot_send, cot_recv
    )
    mine = pl.ds(pl.multiple_of(me * enc, enc), enc)
    cot_ref[mine, :] = cot_src[mine, :]
    stats_here()
    sums = jnp.sum(stat_buf[...], axis=0)
    lane = lax.broadcasted_iota(jnp.int32, (8, c), 1)
    for reach in (1, 2):
        partner = jnp.where(
            lane % (2 * reach) < reach, pltpu.roll(sums, c - reach, 1), pltpu.roll(sums, reach, 1)
        )
        sums = sums + partner
    members = float(n_tm * 2 * height * width * GROUP_SIZE)
    mean = sums[0:1] / members
    variance = sums[1:2] / members - mean * mean
    scale = lax.rsqrt(variance + 1e-06)
    gain, bias = gain_ref[...], bias_ref[...]

    half_w, half_h = width // 2, height // 2
    rows_half = height * half_w

    def hidden_at(parity):
        frames = []
        for t in range(2):
            x = conv_ref[pl.ds(t * height * width + parity, rows_half, stride=2), :]
            y = (x - mean) * scale * gain + bias
            y = y / (1.0 + jnp.exp(-y))
            y = y.astype(jnp.bfloat16).astype(jnp.float32)
            frames.append(y.reshape(half_h, 2, 1, half_w, c))
        return jnp.concatenate(frames, axis=2)

    even, odd = hidden_at(0), hidden_at(1)
    flat = even.reshape(-1, half_w, c)
    place = lax.broadcasted_iota(jnp.int32, flat.shape, 1)
    shifted = jnp.where(place == half_w - 1, 0.0, pltpu.roll(flat, half_w - 1, 1)).reshape(even.shape)
    for q, source in enumerate((even, odd, shifted)):
        upper, lower = source[:, 0], source[:, 1]
        below = jnp.concatenate([upper[1:], jnp.zeros_like(upper[:1])], axis=0)
        for p, rows in enumerate((upper, lower, below)):
            at = (p * 3 + q) * c
            patches[:, at : at + c] = rows.reshape(-1, c).astype(jnp.bfloat16)

    cot_here()
    partial_grad = lax.dot_general(
        cot_ref[...], patches[...], (((0,), (0,)), ((), ())), preferred_element_type=jnp.float32
    )
    for tap in range(9):
        grad_all[tap] = partial_grad[:, tap * c : (tap + 1) * c]
    grad_wide[...] = jnp.zeros_like(grad_wide)
    for tap in range(9):
        for j in range(own):
            grad_wide[pl.ds(tap * own + j, n_tm, stride=piece), :] = grad_all[
                tap, pl.ds(j, n_tm, stride=own), :
            ]
    grad_src[...] = grad_wide[...].astype(jnp.bfloat16)
    grad_here, grad_gone = exchange(
        n_tm, tm_peer, me,
        lambda i: grad_src.at[pl.ds(pl.multiple_of(i * piece, piece), piece)],
        lambda i: grad_buf.at[pl.ds(pl.multiple_of(i * piece, piece), piece)],
        grad_send, grad_recv,
    )
    here = pl.ds(pl.multiple_of(me * piece, piece), piece)
    grad_buf[here, :] = grad_src[here, :]

    enc_src[...] = jnp.dot(
        patches[...], down_ref[...], preferred_element_type=jnp.float32
    ).astype(jnp.bfloat16)
    enc_here, enc_gone = exchange(
        n_tm, tm_peer, me, block_of(enc_src), block_of(enc_buf), enc_send, enc_recv
    )
    enc_buf[mine, :] = enc_src[mine, :]

    grad_here()
    total = jnp.zeros((piece, c), jnp.float32)
    for i in range(n_tm):
        total = total + grad_buf[pl.ds(i * piece, piece), :].astype(jnp.float32)
    x_src[...] = total
    x_buf[my_x] = total
    x_here, x_gone = exchange(
        n_x, x_peer, my_x, lambda i: x_src, lambda i: x_buf.at[i], x_send, x_recv
    )
    x_here()
    total = jnp.sum(x_buf[...], axis=0)
    z_src[...] = total
    z_buf[my_z] = total
    z_here, z_gone = exchange(
        Z_PART, z_peer, my_z, lambda i: z_src, lambda i: z_buf.at[i], z_send, z_recv
    )
    enc_here()
    enc_out[...] = enc_buf[...]
    z_here()
    total = jnp.sum(z_buf[...], axis=0)
    for tap in range(9):
        grad_out[tap] = total[tap * own : (tap + 1) * own]
    for gone in (stats_gone, cot_gone, grad_gone, enc_gone, x_gone, z_gone):
        gone()


def per_device(activations, conv_weight, norm_gain, norm_bias, down_weight, cotangent):
    _, frames_dev, height, width, c = activations.shape
    n_tm, n_dp = lax.axis_size("tm"), lax.axis_size("dp")
    cells = height * width
    positions = frames_dev * cells // 4
    own = c // n_tm
    piece = -(-9 * own // 16) * 16
    earlier = passed_along(activations, "tm", 1)
    f32, bf16 = jnp.float32, jnp.bfloat16
    n_x = n_dp // Z_PART
    dma = pltpu.SemaphoreType.DMA
    encoded, grad = pl.pallas_call(
        functools.partial(block_kernel, n_tm, n_dp, height, width, piece),
        out_shape=(
            jax.ShapeDtypeStruct((positions, c), bf16),
            jax.ShapeDtypeStruct((9, own, c), f32),
        ),
        in_specs=[VMEM] * 7,
        out_specs=(VMEM, VMEM),
        scratch_shapes=[
            pltpu.VMEM((cells + 2 * width, 4 * c), bf16),
            pltpu.VMEM((3, 4 * c, 6 * c), bf16),
            pltpu.VMEM((frames_dev * cells, c), f32),
            pltpu.VMEM((positions, c), bf16),
            pltpu.VMEM((8, c), f32),
            pltpu.VMEM((n_tm, 8, c), f32),
            pltpu.VMEM((positions, 9 * c), bf16),
            pltpu.VMEM((positions, c), bf16),
            pltpu.VMEM((positions, c), bf16),
            pltpu.VMEM((9, c, c), f32),
            pltpu.VMEM((n_tm * piece, c), f32),
            pltpu.VMEM((n_tm * piece, c), bf16),
            pltpu.VMEM((n_tm * piece, c), bf16),
            pltpu.VMEM((piece, c), f32),
            pltpu.VMEM((n_x, piece, c), f32),
            pltpu.VMEM((piece, c), f32),
            pltpu.VMEM((Z_PART, piece, c), f32),
        ]
        + [dma((n_tm,))] * 8
        + [dma((n_x,))] * 2
        + [dma((Z_PART,))] * 2,
        compiler_params=pltpu.CompilerParams(
            collective_id=0, has_side_effects=True, vmem_limit_bytes=40 << 20
        ),
        name="block",
    )(
        earlier.reshape(frames_dev, cells, c),
        activations.reshape(frames_dev, cells, c),
        conv_weight,
        norm_gain.reshape(1, c),
        norm_bias.reshape(1, c),
        down_weight.reshape(9 * c, c),
        cotangent.reshape(positions, c),
    )
    grad_down = grad.transpose(0, 2, 1).reshape(3, 3, c, own)
    return encoded.reshape(cotangent.shape), grad_down


def solution(mesh):
    placed = (P("dp", "tm", None, None, None), P(), P(), P(), P(), P("dp", None, "tm", None, None))
    return jax.shard_map(
        per_device,
        mesh=mesh,
        in_specs=placed,
        out_specs=(P("dp", None, "tm", None, None), P(None, None, None, "tm")),
        check_vma=False,
    )
```
